32 devices in a mesh: wa: 2 (over x), ha: 16 (over z, y, core).
Axes of the slice: x: 2, y: 2, z: 4, core: 2. Of those that a mesh axis runs over, the one named last changes fastest.
Arguments:
- tokens: float32 [128, 5376], P('ha', 'wa'), may hold values from -6 to 6
- grad_out: float32 [128, 5376], P('ha', 'wa'), may hold values from -1.5 to 1.5
- gate_weight: float32 [5376, 10752], P('wa', 'ha'), may hold values from -0.078125 to 0.078125
- up_weight: float32 [5376, 10752], P('wa', 'ha'), may hold values from -0.078125 to 0.078125
- down_weight: float32 [10752, 5376], P('ha', 'wa'), may hold values from -0.0625 to 0.0625
Outputs:
- grad_tokens: float32 [128, 5376], P('ha', 'wa')
- grad_gate: float32 [5376, 10752], P('wa', 'ha')
- grad_up: float32 [5376, 10752], P('wa', 'ha')
- grad_down: float32 [10752, 5376], P('ha', 'wa')
The draws below stay inside these ranges and needn't reach their ends.
All inputs are finite; a program needn't handle non-finite values.
Results may differ from the reference program's by a relative error of at most 0.00018.
Values sent between devices are 32-bit elements; how exact they have to be, the bound alone decides.
No kernel may reach another device: no remote copies, remote signals or barrier semaphores. Data moves between devices by JAX's collectives and lax.ppermute only.
A program may use at most 128 MiB of HBM per device.

```python
import jax
import jax.numpy as jnp
from jax import lax

D = 5376
FF = 10752
TOKENS = 128


def levels(stream_key, extent, shards, least, top_value):
    loudness, own = 1.0, jax.random.fold_in(stream_key, 6)
    for position, shards_of in shards:
        steps = jnp.exp(jax.random.uniform(jax.random.fold_in(own, position), (shards_of,), jnp.float32, least / len(shards), top_value / len(shards)))
        loudness = loudness * jnp.repeat(steps, extent[position] // shards_of).reshape([-1 if axis == position else 1 for axis in range(len(extent))])
    return loudness


def gaussian(key, extent, width, most, shards=(), dtype=jnp.bfloat16):
    gain = levels(key, extent, shards, -0.22, 0.18) if shards else 1.0
    entries = jax.random.normal(key, extent, jnp.float32) * width * gain
    return jnp.minimum(jnp.maximum(entries, -most), most).astype(dtype)


def setup_inputs(seed: int = 0) -> dict:
    key_of = jax.random.split(jax.random.key(seed), 6)
    return {
        "tokens": gaussian(key_of[0], (TOKENS, D), 1.0, 6.0, ((0, 16), (1, 2)), jnp.float32),
        "grad_out": gaussian(key_of[1], (TOKENS, D), 0.25, 1.5, ((0, 16), (1, 2)), jnp.float32),
        "gate_weight": gaussian(key_of[2], (D, FF), D ** -0.5, 0.078125, ((0, 2), (1, 16)), jnp.float32),
        "up_weight": gaussian(key_of[3], (D, FF), D ** -0.5, 0.078125, ((0, 2), (1, 16)), jnp.float32),
        "down_weight": gaussian(key_of[4], (FF, D), FF ** -0.5, 0.0625, ((0, 16), (1, 2)), jnp.float32),
    }


def matmul(left, right):
    return jnp.dot(left, right, preferred_element_type=jnp.float32, precision=lax.Precision.HIGHEST)


def reference(tokens, grad_out, gate_weight, up_weight, down_weight):
    gate = matmul(tokens, gate_weight)
    up = matmul(tokens, up_weight)
    grad_hidden = matmul(grad_out, down_weight.T)
    sig = 1.0 / (1.0 + jnp.exp(-gate))
    hidden = gate * sig * up
    grad_up_act = grad_hidden * gate * sig
    grad_gate_act = grad_hidden * up * sig * (1.0 + gate * (1.0 - sig))
    grad_down = matmul(hidden.T, grad_out)
    grad_gate = matmul(tokens.T, grad_gate_act)
    grad_up = matmul(tokens.T, grad_up_act)
    grad_tokens = matmul(grad_gate_act, gate_weight.T) + matmul(grad_up_act, up_weight.T)
    return grad_tokens, grad_gate, grad_up, grad_down
```

```python
import jax
import jax.numpy as jnp
from jax import lax
from jax.sharding import PartitionSpec as P


def contract(left, right, left_dim, right_dim):
    return lax.dot_general(
        left,
        right,
        (((left_dim,), (right_dim,)), ((), ())),
        preferred_element_type=jnp.float32,
        precision=lax.Precision.HIGH,
    )


def derivs(gate, up, grad_hidden):
    sig = 1.0 / (1.0 + jnp.exp(-gate))
    hidden = gate * sig * up
    grad_up_act = grad_hidden * gate * sig
    grad_gate_act = grad_hidden * up * sig * (1.0 + gate * (1.0 - sig))
    return (hidden, grad_gate_act, grad_up_act)


def swap(x, axis, size, bit):
    return lax.ppermute(x, axis, [(i, i ^ bit) for i in range(size)])


def bits_of(size):
    assert size & (size - 1) == 0
    return [1 << b for b in reversed(range(size.bit_length() - 1))]


def gather(x, axis, size):
    for bit in bits_of(size):
        x = jnp.concatenate([x, swap(x, axis, size, bit)], axis=0)
    return x


def scatter_sum(x, axis, size):
    for bit in reversed(bits_of(size)):
        half = x.shape[0] // 2
        x = x[:half] + swap(x[half:], axis, size, bit)
    return x


def all_sum(x, axis, size):
    for bit in bits_of(size):
        x = x + swap(x, axis, size, bit)
    return x


def solution(mesh):
    nw, nh = mesh.shape["wa"], mesh.shape["ha"]

    def per_device(tokens, grad_out, gate_weight, up_weight, down_weight):
        inputs = gather(tokens, "ha", nh)
        upstream = gather(grad_out, "ha", nh)
        gate = all_sum(contract(inputs, gate_weight, 1, 0), "wa", nw)
        up = all_sum(contract(inputs, up_weight, 1, 0), "wa", nw)
        grad_hidden = all_sum(contract(upstream, down_weight, 1, 1), "wa", nw)
        hidden, grad_gate_act, grad_up_act = derivs(gate, up, grad_hidden)
        grad_tokens = scatter_sum(
            contract(grad_gate_act, gate_weight, 1, 1) + contract(grad_up_act, up_weight, 1, 1),
            "ha",
            nh,
        )
        grad_down = contract(hidden, upstream, 0, 0)
        grad_gate = contract(inputs, grad_gate_act, 0, 0)
        grad_up = contract(inputs, grad_up_act, 0, 0)
        return (grad_tokens, grad_gate, grad_up, grad_down)

    placed = (P("ha", "wa"), P("ha", "wa"), P("wa", "ha"), P("wa", "ha"), P("ha", "wa"))
    return jax.shard_map(
        per_device,
        mesh=mesh,
        in_specs=placed,
        out_specs=(P("ha", "wa"), P("wa", "ha"), P("wa", "ha"), P("ha", "wa")),
        check_vma=False,
    )
```
